32 devices in a mesh: groups: 2 (over y), replica: 4 (over z), tensor: 4 (over x, core).
Axes of the slice: x: 2, y: 2, z: 4, core: 2. Of those that a mesh axis runs over, the one named last changes fastest.
Arguments:
- queries: bfloat16 [512, 64, 128], P(('groups', 'replica'), 'tensor'), parts along dimension 0, may hold values from -256 to 256
- prefix_pool: bfloat16 [16, 64, 2, 8, 128], P(('groups', 'replica'), None, None, 'tensor'), parts along dimension 0, may hold values from -8 to 8
- page_table: int32 [12], P('groups'), parts along dimension 0, may hold values from 0 to 7, as said below
- suffix_kv: bfloat16 [512, 24, 2, 8, 128], P(('groups', 'replica'), None, None, 'tensor'), parts along dimension 0, may hold values from -9 to 9
- new_kv: bfloat16 [512, 2, 8, 128], P(('groups', 'replica'), None, 'tensor'), parts along dimension 0, may hold values from -10 to 10
- suffix_len: int32 [512], P(('groups', 'replica')), parts along dimension 0, may hold values from 0 to 24
- counts: int32 [8], P(('groups', 'replica')), parts along dimension 0, may hold values from 0 to 64, as said below
Outputs:
- attended: bfloat16 [512, 64, 128], P(('groups', 'replica'), 'tensor'), parts along dimension 0
The draws below stay inside these ranges and needn't reach their ends.
There are 2 independent parts, one for each index of `groups`. The reference program is written for one: setup_inputs(seed, part) draws one part's arguments, and reference() takes and returns one part's arrays. A program takes and returns all parts, laid end to end along the dimension named above; each array names one. Nothing has to cross between parts.
Inputs may be any that keep to these rules, and one draw needn't show every extreme that they name: `page_table`: 6 distinct pool slots, among them slots 0 and 7. The counts of replicas 2i and 2i + 1 sum to 64.
All inputs are finite; a program needn't handle non-finite values.
Results may differ from the reference program's by a relative error of at most 0.013.
Values may be sent and summed in bfloat16 or wider, within the bound.
A program may use at most 64 MiB of HBM per device.

```python
import jax
import jax.numpy as jnp
from jax import lax

QH = 64
KVH = 8
HD = 128
PAGE = 64
BAL = 32
SUF = 24
CAP = 64
REQ = 256
SLOTS = 8
PAGES = 6
N_REPLICA = 4


def make_pool(pool_key):
    normal_base = jax.random.normal(pool_key, (SLOTS, PAGE, 2, KVH, HD), jnp.float32)
    return jnp.clip(normal_base, -6.0, 6.0)


def draw_prefix_pool(key, part):
    normal_base = make_pool(jax.random.fold_in(key, 11))
    return normal_base.astype(jnp.bfloat16)


def draw_queries(key, part):
    drawn_draw = jnp.clip(jax.random.normal(jax.random.fold_in(key, 23), (REQ, QH, HD), jnp.float32) * 2.5, -15.0, 15.0)
    return drawn_draw.astype(jnp.bfloat16)


def draw_page_table(key, part):
    first_key, second_key = jax.random.split(jax.random.fold_in(key, 37))
    middle_slots = 1 + jax.random.permutation(first_key, SLOTS - 2)[:PAGES - 2]
    chosen = jnp.concatenate([jnp.array([0, SLOTS - 1], jnp.int32), middle_slots.astype(jnp.int32)])
    return jax.random.permutation(second_key, chosen).astype(jnp.int32)


def draw_counts(key, part):
    pair_count = N_REPLICA // 2
    load_key, full_key, order_key = jax.random.split(jax.random.fold_in(key, 53), 3)
    heavy_load = jax.random.randint(load_key, (pair_count,), BAL, CAP + 1)
    full_pair = jax.random.randint(full_key, (), 0, pair_count)
    heavy_load = jnp.where(jnp.arange(pair_count) == full_pair, CAP, heavy_load)
    heavy_first = jax.random.randint(order_key, (pair_count,), 0, 2)
    even_load = jnp.where(heavy_first == 1, heavy_load, CAP - heavy_load)
    return jnp.stack([even_load, CAP - even_load], axis=1).reshape(N_REPLICA).astype(jnp.int32)


def place_ends(values, rng, smallest, high):
    extent = values.shape
    index_at = [jax.random.randint(jax.random.fold_in(rng, axis), (), 0, extent[axis]) for axis in range(len(extent))]
    values = values.at[tuple(index_at)].set(smallest)
    longest = extent.index(max(extent))
    index_at[longest] = (index_at[longest] + 1) % extent[longest]
    return values.at[tuple(index_at)].set(high)


def block_levels(key, shape, cuts, least, high):
    loudness, own = 1.0, jax.random.fold_in(key, 6)
    for position, blocks in cuts:
        steps = jnp.exp(jax.random.uniform(jax.random.fold_in(own, position), (blocks,), jnp.float32, least / len(cuts), high / len(cuts)))
        loudness = loudness * jnp.repeat(steps, shape[position] // blocks).reshape([-1 if axis == position else 1 for axis in range(len(shape))])
    return loudness


def scatter_about(own_key, extent, spread, most, cuts=(), held_as=jnp.bfloat16):
    level = block_levels(own_key, extent, cuts, -0.22, 0.18) if cuts else 1.0
    drawn = jax.random.normal(own_key, extent, jnp.float32) * spread * level
    return jnp.minimum(jnp.maximum(drawn, -most), most).astype(held_as)


def setup_inputs(seed: int = 0, part: int = 0) -> dict:
    arg_keys = jax.random.split(jax.random.key(seed), 8)
    part_keys = jax.random.split(jax.random.fold_in(arg_keys[7], part), 8)
    queries = draw_queries(jax.random.fold_in(jax.random.fold_in(arg_keys[7], part), 71), part)
    prefix_pool = draw_prefix_pool(jax.random.fold_in(jax.random.fold_in(arg_keys[7], part), 71), part)
    page_table = draw_page_table(jax.random.fold_in(jax.random.fold_in(arg_keys[7], part), 71), part)
    suffix_kv = scatter_about(part_keys[3], (REQ, SUF, 2, KVH, HD), 1.5, 9.0, ((0, 4), (3, 4)))
    new_kv = scatter_about(part_keys[4], (REQ, 2, KVH, HD), 1.7, 10.0, ((0, 4), (2, 4)))
    suffix_len = place_ends(jax.random.randint(part_keys[5], (REQ,), 0, SUF + 1), jax.random.fold_in(part_keys[5], 1), 0, SUF).astype(jnp.int32)
    counts = draw_counts(jax.random.fold_in(jax.random.fold_in(arg_keys[7], part), 71), part)
    return {"queries": queries, "prefix_pool": prefix_pool, "page_table": page_table, "suffix_kv": suffix_kv, "new_kv": new_kv, "suffix_len": suffix_len, "counts": counts}


masked_score = -1.0e30


def rounded_copy(values):
    return lax.optimization_barrier(values.astype(jnp.bfloat16)).astype(jnp.float32)


def reference(queries, prefix_pool, page_table, suffix_kv, new_kv, suffix_len, counts):
    group = QH // KVH
    factor_q = HD ** -0.5
    live_pool = prefix_pool[page_table.astype(jnp.int32)].reshape(PAGES * PAGE, 2, KVH, HD).astype(jnp.float32)
    prefix_keys = live_pool[:, 0]
    prefix_values = live_pool[:, 1]

    def one_block(block_item):
        block_q, block_suffix, block_new, block_len, block_count = block_item
        grouped = block_q.astype(jnp.float32).reshape(CAP, KVH, group, HD)
        suffix_all = block_suffix.astype(jnp.float32)
        new_all = block_new.astype(jnp.float32)
        prefix_scores = jnp.einsum("rgqd,kgd->rgqk", grouped, prefix_keys) * factor_q
        suffix_scores = jnp.einsum("rgqd,rkgd->rgqk", grouped, suffix_all[:, :, 0]) * factor_q
        kept_keys = jnp.arange(SUF, dtype=jnp.int32)[None, :] < block_len[:, None]
        suffix_scores = jnp.where(kept_keys[:, None, None, :], suffix_scores, masked_score)
        new_score = jnp.einsum("rgqd,rgd->rgq", grouped, new_all[:, 0]) * factor_q
        row_max = jnp.maximum(jnp.maximum(jnp.max(prefix_scores, axis=-1), jnp.max(suffix_scores, axis=-1)), new_score)
        prefix_weights = jnp.exp(prefix_scores - row_max[..., None])
        suffix_weights = jnp.exp(suffix_scores - row_max[..., None])
        new_weight = jnp.exp(new_score - row_max)
        row_total = jnp.sum(prefix_weights, axis=-1) + jnp.sum(suffix_weights, axis=-1) + new_weight
        accumulated = jnp.einsum("rgqk,kgd->rgqd", rounded_copy(prefix_weights), prefix_values)
        accumulated = accumulated + jnp.einsum("rgqk,rkgd->rgqd", rounded_copy(suffix_weights), suffix_all[:, :, 1])
        accumulated = accumulated + rounded_copy(new_weight)[..., None] * new_all[:, 1][:, :, None, :]
        result = accumulated / row_total[..., None]
        live_rows = jnp.arange(CAP, dtype=jnp.int32) < block_count
        result = jnp.where(live_rows[:, None, None, None], result, 0.0)
        return result.reshape(CAP, QH, HD).astype(jnp.bfloat16)

    blocks = (
        queries.reshape(N_REPLICA, CAP, QH, HD),
        suffix_kv.reshape(N_REPLICA, CAP, SUF, 2, KVH, HD),
        new_kv.reshape(N_REPLICA, CAP, 2, KVH, HD),
        suffix_len.reshape(N_REPLICA, CAP),
        counts,
    )
    return lax.map(one_block, blocks).reshape(REQ, QH, HD)
```

```python
import functools
import math

import jax
import jax.numpy as jnp
from jax import lax
from jax.experimental import pallas as pl
from jax.experimental.pallas import tpu as pltpu
from jax.sharding import PartitionSpec as P

masked_score = -1e30
MESH = pl.DeviceIdType.MESH
SB = 8


def kernel(n, dims, table_ref, len_ref, count_ref, q_hbm, pool_hbm, suf_hbm, new_hbm, out_ref,
           gather, q_in, suf, new, perm, qs, knew, vnew, kx, vx, m_ref, acc_ref,
           local_sem, send_sem, recv_sem):
    rows, heads, kv_heads, depth, suf_len, page, slots, chunks = dims
    group = heads // kv_heads
    per_token = 2 * kv_heads
    scale = (1.0 / math.sqrt(depth)) * math.log2(math.e)
    block_rows = slots * page * per_token
    chunk_rows = block_rows // chunks
    tile_tokens = page
    tile_rows = page * per_token
    keys = slots * page
    me = lax.axis_index("replica")
    has_left, has_right = me > 0, me < n - 1

    barrier = pltpu.get_barrier_semaphore()

    @pl.when(has_left)
    def _():
        pl.semaphore_signal(barrier, inc=1, device_id={"replica": me - 1}, device_id_type=MESH)

    @pl.when(has_right)
    def _():
        pl.semaphore_signal(barrier, inc=1, device_id={"replica": me + 1}, device_id_type=MESH)

    copies = [
        pltpu.make_async_copy(q_hbm, q_in, local_sem.at[0]),
        pltpu.make_async_copy(new_hbm, new, local_sem.at[1]),
        pltpu.make_async_copy(suf_hbm, suf, local_sem.at[2]),
        pltpu.make_async_copy(pool_hbm, gather.at[me], local_sem.at[3]),
    ]
    for copy in copies:
        copy.start()

    out_row = lax.broadcasted_iota(jnp.int32, (tile_rows, tile_rows), 0)
    in_row = lax.broadcasted_iota(jnp.int32, (tile_rows, tile_rows), 1)
    source = lax.rem(out_row, page) * per_token + lax.div(out_row, page)
    perm[...] = jnp.where(in_row == source, 1.0, 0.0).astype(jnp.bfloat16)

    pl.semaphore_wait(barrier, has_left.astype(jnp.int32) + has_right.astype(jnp.int32))

    def send(direction, block, chunk, own):
        at = pl.ds(chunk * chunk_rows, chunk_rows)
        return pltpu.make_async_remote_copy(
            src_ref=pool_hbm.at[at] if own else gather.at[block, at],
            dst_ref=gather.at[block, at],
            send_sem=send_sem.at[direction, block, chunk],
            recv_sem=recv_sem.at[block, chunk],
            device_id={"replica": me + 1 if direction == 0 else me - 1},
            device_id_type=MESH,
        )

    for chunk in range(chunks):
        @pl.when(has_right)
        def _():
            send(0, me, chunk, True).start()

        @pl.when(has_left)
        def _():
            send(1, me, chunk, True).start()

    def relay(step, chunk):
        @pl.when(me - step >= 0)
        def _():
            send(0, me - step, chunk, False).wait_recv()

            @pl.when(has_right)
            def _():
                send(0, me - step, chunk, False).start()

        @pl.when(me + step < n)
        def _():
            send(1, me + step, chunk, False).wait_recv()

            @pl.when(has_left)
            def _():
                send(1, me + step, chunk, False).start()

    def split(block):
        return jnp.dot(perm[...], block, preferred_element_type=jnp.float32).astype(jnp.bfloat16)

    def piece(parts, which, head):
        at = (which * kv_heads + head) * page
        return parts[at : at + page]

    copies[0].wait()
    copies[1].wait()
    queries = q_in[...].astype(jnp.float32).reshape(rows, kv_heads, group, depth)
    for head in range(kv_heads):
        qs[head] = queries[:, head].reshape(rows * group, depth).astype(jnp.bfloat16)
    fresh = split(new[...])
    for head in range(kv_heads):
        knew[head] = piece(fresh, 0, head)
        vnew[head] = piece(fresh, 1, head)
    copies[2].wait()

    block_keys = SB * suf_len
    width = block_keys + rows
    tiles = block_keys // tile_tokens
    part = SB * group

    def suffix_block(index):
        columns = lax.broadcasted_iota(jnp.int32, (group, width), 1)
        masks = []
        for at in range(SB):
            low = at * suf_len
            high = low + len_ref[index * SB + at]
            own = (columns >= low) & (columns < high)
            masks.append(own | (columns == block_keys + index * SB + at))
        parts = [
            split(suf[pl.ds(pl.multiple_of((index * tiles + t) * tile_rows, tile_rows), tile_rows), :])
            for t in range(tiles)
        ]
        ones = jnp.ones((width, depth), jnp.bfloat16)
        at = pl.ds(pl.multiple_of(index * part, part), part)
        for head in range(kv_heads):
            key = jnp.concatenate([piece(p, 0, head) for p in parts] + [knew[head]], axis=0)
            value = jnp.concatenate([piece(p, 1, head) for p in parts] + [vnew[head]], axis=0)
            value = jnp.concatenate([value, ones], axis=1)
            scores = lax.dot_general(
                qs[head, at, :], key, (((1,), (1,)), ((), ())), preferred_element_type=jnp.float32
            )
            scores = jnp.concatenate(
                [
                    jnp.where(masks[i], scores[i * group : (i + 1) * group], masked_score)
                    for i in range(SB)
                ],
                axis=0,
            )
            top = jnp.max(scores, axis=1, keepdims=True)
            weights = jnp.exp2((scores - top) * scale).astype(jnp.bfloat16)
            acc_ref[head, at, :] = jnp.dot(weights, value, preferred_element_type=jnp.float32)
            m_ref[head, at, :] = jnp.broadcast_to(top, (part, depth))

    def prepare(side, block):
        parts = [split(gather[block, s * tile_rows : (s + 1) * tile_rows, :]) for s in range(slots)]
        for head in range(kv_heads):
            kx[side, head] = jnp.concatenate([piece(p, 0, head) for p in parts], axis=0)
            vx[side, head, :, :depth] = jnp.concatenate([piece(p, 1, head) for p in parts], axis=0)

    def slot_live(slot):
        def look(at, found):
            return found | (table_ref[at] == slot).astype(jnp.int32)

        pages = table_ref.shape[0]
        if pages <= 16:
            found = jnp.int32(0)
            for at in range(pages):
                found = look(at, found)
            return found
        return lax.fori_loop(0, pages, look, jnp.int32(0))

    quarter = rows * group // chunks

    def prefix_part(side, block, which):
        columns = lax.broadcasted_iota(jnp.int32, (1, keys), 1)
        live = jnp.zeros((1, keys), jnp.int32)
        for s in range(slots):
            inside = (columns >= s * page) & (columns < (s + 1) * page)
            live = jnp.where(inside, slot_live(block * slots + s), live)
        at = pl.ds(which * quarter, quarter)
        for head in range(kv_heads):
            scores = lax.dot_general(
                qs[head, at, :], kx[side, head], (((1,), (1,)), ((), ())),
                preferred_element_type=jnp.float32,
            )
            scores = jnp.where(live > 0, scores, masked_score)
            before = m_ref[head, at, :]
            top = jnp.maximum(before, jnp.max(scores, axis=1, keepdims=True))
            factor = jnp.exp2((before - top) * scale)
            weights = jnp.exp2((scores - top[:, :1]) * scale).astype(jnp.bfloat16)
            added = jnp.dot(weights, vx[side, head], preferred_element_type=jnp.float32)
            acc_ref[head, at, :depth] = acc_ref[head, at, :depth] * factor + added[:, :depth]
            acc_ref[head, at, depth:] = acc_ref[head, at, depth:] * factor + added[:, depth:]
            m_ref[head, at, :] = top

    def absorb(step, which):
        if isinstance(step, int) and step == 0:
            if which == 0:
                prepare(0, me)
            prefix_part(0, me, which)
            return

        @pl.when(me - step >= 0)
        def _():
            if which == 0:
                prepare(0, me - step)
            prefix_part(0, me - step, which)

        @pl.when(me + step < n)
        def _():
            if which == 0:
                prepare(1, me + step)
            prefix_part(1, me + step, which)

    for side in range(2):
        for head in range(kv_heads):
            vx[side, head, :, depth:] = jnp.ones((keys, depth), jnp.bfloat16)

    suffix_blocks = rows // SB
    early = suffix_blocks // 2
    late = (suffix_blocks - early) // chunks

    def run_suffix(first, count):
        def body(index, carry):
            suffix_block(first + index)
            return carry

        lax.fori_loop(0, count, body, 0)

    run_suffix(0, suffix_blocks - late * chunks)
    copies[3].wait()
    for chunk in range(chunks):
        relay(1, chunk)
        run_suffix(suffix_blocks - late * (chunks - chunk), late)
    for chunk in range(chunks):
        absorb(0, chunk)

    def step_body(step):
        for chunk in range(chunks):
            relay(step, chunk)
            absorb(step - 1, chunk)

    if n <= 8:
        for step in range(2, n):
            step_body(step)
    else:
        def loop(step, carry):
            step_body(step)
            return carry

        lax.fori_loop(2, n, loop, 0)
    for chunk in range(chunks):
        absorb(n - 1, chunk)

    span = rows // chunks
    count = count_ref[0]
    for chunk in range(chunks):
        at = pl.ds(chunk * quarter, quarter)
        heads_out = [
            (acc_ref[head, at, :depth] / acc_ref[head, at, depth:]).reshape(span, group, depth)
            for head in range(kv_heads)
        ]
        result = jnp.concatenate(heads_out, axis=1)
        row = lax.broadcasted_iota(jnp.int32, result.shape, 0) + chunk * span
        result = jnp.where(row < count, result, 0.0)
        out_ref[pl.ds(chunk * span, span)] = result.astype(jnp.bfloat16)

    def drain(block):
        for chunk in range(chunks):
            @pl.when(has_right & (block <= me))
            def _():
                send(0, block, chunk, False).wait_send()

            @pl.when(has_left & (block >= me))
            def _():
                send(1, block, chunk, False).wait_send()

    if n <= 8:
        for block in range(n):
            drain(block)
    else:
        def drain_loop(block, carry):
            drain(block)
            return carry

        lax.fori_loop(0, n, drain_loop, 0)


def shards(n, queries, prefix_pool, page_table, suffix_kv, new_kv, suffix_len, counts):
    rows, heads, depth = queries.shape
    slots, page, pair, kv_heads, depth = prefix_pool.shape
    suf_len = suffix_kv.shape[1]
    chunks = 4 if n <= 8 else 2
    group = heads // kv_heads
    dims = (rows, heads, kv_heads, depth, suf_len, page, slots, chunks)
    pool = prefix_pool.reshape(slots * page * 2 * kv_heads, depth)
    suffix = suffix_kv.reshape(rows * suf_len * 2 * kv_heads, depth)
    new = new_kv.reshape(rows * 2 * kv_heads, depth)
    tile_rows = page * 2 * kv_heads
    bf, f32 = jnp.bfloat16, jnp.float32
    anywhere = pl.BlockSpec(memory_space=pl.ANY)
    scalars = pl.BlockSpec(memory_space=pltpu.SMEM)
    return pl.pallas_call(
        functools.partial(kernel, n, dims),
        name="attend",
        out_shape=jax.ShapeDtypeStruct((rows, heads, depth), bf),
        in_specs=[scalars] * 3 + [anywhere] * 4,
        out_specs=pl.BlockSpec(memory_space=pltpu.VMEM),
        scratch_shapes=[
            pltpu.VMEM((n,) + pool.shape, bf),
            pltpu.VMEM(queries.shape, bf),
            pltpu.VMEM(suffix.shape, bf),
            pltpu.VMEM(new.shape, bf),
            pltpu.VMEM((tile_rows, tile_rows), bf),
            pltpu.VMEM((kv_heads, rows * group, depth), bf),
            pltpu.VMEM((kv_heads, rows, depth), bf),
            pltpu.VMEM((kv_heads, rows, depth), bf),
            pltpu.VMEM((2, kv_heads, slots * page, depth), bf),
            pltpu.VMEM((2, kv_heads, slots * page, 2 * depth), bf),
            pltpu.VMEM((kv_heads, rows * group, depth), f32),
            pltpu.VMEM((kv_heads, rows * group, 2 * depth), f32),
            pltpu.SemaphoreType.DMA((4,)),
            pltpu.SemaphoreType.DMA((2, n, chunks)),
            pltpu.SemaphoreType.DMA((n, chunks)),
        ],
        compiler_params=pltpu.CompilerParams(collective_id=0, has_side_effects=True),
    )(page_table, suffix_len, counts, queries, pool, suffix, new)


def solution(mesh):
    placed = (
        P(("groups", "replica"), "tensor", None),
        P(("groups", "replica"), None, None, "tensor", None),
        P("groups"),
        P(("groups", "replica"), None, None, "tensor", None),
        P(("groups", "replica"), None, "tensor", None),
        P(("groups", "replica")),
        P(("groups", "replica")),
    )
    return jax.shard_map(
        functools.partial(shards, mesh.shape["replica"]),
        mesh=mesh,
        in_specs=placed,
        out_specs=P(("groups", "replica"), "tensor", None),
        check_vma=False,
    )
```

```python
import functools
import math

import jax
import jax.numpy as jnp
from jax import lax
from jax.experimental import pallas as pl
from jax.experimental.pallas import tpu as pltpu
from jax.sharding import PartitionSpec as P

masked_score = -1e30
MESH = pl.DeviceIdType.MESH
SB = 8


def kernel(n, dims, table_hbm, len_hbm, count_hbm, q_hbm, pool_hbm, suf_hbm, new_hbm, out_ref,
           table_ref, len_ref, count_ref, gather, q_in, suf, new, perm, qs, knew, vnew, kx, vx, m_ref, acc_ref,
           local_sem, send_sem, recv_sem):
    rows, heads, kv_heads, depth, suf_len, page, slots, chunks = dims
    group = heads // kv_heads
    per_token = 2 * kv_heads
    scale = (1.0 / math.sqrt(depth)) * math.log2(math.e)
    block_rows = slots * page * per_token
    chunk_rows = block_rows // chunks
    tile_tokens = page
    tile_rows = page * per_token
    keys = slots * page
    me = lax.axis_index("replica")
    has_left, has_right = me > 0, me < n - 1

    barrier = pltpu.get_barrier_semaphore()

    @pl.when(has_left)
    def _():
        pl.semaphore_signal(barrier, inc=1, device_id={"replica": me - 1}, device_id_type=MESH)

    @pl.when(has_right)
    def _():
        pl.semaphore_signal(barrier, inc=1, device_id={"replica": me + 1}, device_id_type=MESH)

    copies = [
        pltpu.make_async_copy(q_hbm, q_in, local_sem.at[0]),
        pltpu.make_async_copy(new_hbm, new, local_sem.at[1]),
        pltpu.make_async_copy(suf_hbm, suf, local_sem.at[2]),
        pltpu.make_async_copy(pool_hbm, gather.at[me], local_sem.at[3]),
        pltpu.make_async_copy(table_hbm, table_ref, local_sem.at[4]),
        pltpu.make_async_copy(len_hbm, len_ref, local_sem.at[5]),
        pltpu.make_async_copy(count_hbm, count_ref, local_sem.at[6]),
    ]
    for copy in copies:
        copy.start()

    out_row = lax.broadcasted_iota(jnp.int32, (tile_rows, tile_rows), 0)
    in_row = lax.broadcasted_iota(jnp.int32, (tile_rows, tile_rows), 1)
    source = lax.rem(out_row, page) * per_token + lax.div(out_row, page)
    perm[...] = jnp.where(in_row == source, 1.0, 0.0).astype(jnp.bfloat16)

    pl.semaphore_wait(barrier, has_left.astype(jnp.int32) + has_right.astype(jnp.int32))

    def send(direction, block, chunk, own):
        at = pl.ds(chunk * chunk_rows, chunk_rows)
        return pltpu.make_async_remote_copy(
            src_ref=pool_hbm.at[at] if own else gather.at[block, at],
            dst_ref=gather.at[block, at],
            send_sem=send_sem.at[direction, block, chunk],
            recv_sem=recv_sem.at[block, chunk],
            device_id={"replica": me + 1 if direction == 0 else me - 1},
            device_id_type=MESH,
        )

    for chunk in range(chunks):
        @pl.when(has_right)
        def _():
            send(0, me, chunk, True).start()

        @pl.when(has_left)
        def _():
            send(1, me, chunk, True).start()

    def relay(step, chunk):
        @pl.when(me - step >= 0)
        def _():
            send(0, me - step, chunk, False).wait_recv()

            @pl.when(has_right)
            def _():
                send(0, me - step, chunk, False).start()

        @pl.when(me + step < n)
        def _():
            send(1, me + step, chunk, False).wait_recv()

            @pl.when(has_left)
            def _():
                send(1, me + step, chunk, False).start()

    def split(block):
        return jnp.dot(perm[...], block, preferred_element_type=jnp.float32).astype(jnp.bfloat16)

    def piece(parts, which, head):
        at = (which * kv_heads + head) * page
        return parts[at : at + page]

    copies[0].wait()
    copies[1].wait()
    queries = q_in[...].astype(jnp.float32).reshape(rows, kv_heads, group, depth)
    for head in range(kv_heads):
        qs[head] = queries[:, head].reshape(rows * group, depth).astype(jnp.bfloat16)
    fresh = split(new[...])
    for head in range(kv_heads):
        knew[head] = piece(fresh, 0, head)
        vnew[head] = piece(fresh, 1, head)
    copies[2].wait()
    for copy in copies[4:]:
        copy.wait()

    block_keys = SB * suf_len
    width = block_keys + rows
    tiles = block_keys // tile_tokens
    part = SB * group

    def suffix_block(index):
        columns = lax.broadcasted_iota(jnp.int32, (group, width), 1)
        masks = []
        for at in range(SB):
            low = at * suf_len
            high = low + len_ref[index * SB + at]
            own = (columns >= low) & (columns < high)
            masks.append(own | (columns == block_keys + index * SB + at))
        parts = [
            split(suf[pl.ds(pl.multiple_of((index * tiles + t) * tile_rows, tile_rows), tile_rows), :])
            for t in range(tiles)
        ]
        ones = jnp.ones((width, depth), jnp.bfloat16)
        at = pl.ds(pl.multiple_of(index * part, part), part)
        for head in range(kv_heads):
            key = jnp.concatenate([piece(p, 0, head) for p in parts] + [knew[head]], axis=0)
            value = jnp.concatenate([piece(p, 1, head) for p in parts] + [vnew[head]], axis=0)
            value = jnp.concatenate([value, ones], axis=1)
            scores = lax.dot_general(
                qs[head, at, :], key, (((1,), (1,)), ((), ())), preferred_element_type=jnp.float32
            )
            scores = jnp.concatenate(
                [
                    jnp.where(masks[i], scores[i * group : (i + 1) * group], masked_score)
                    for i in range(SB)
                ],
                axis=0,
            )
            top = jnp.max(scores, axis=1, keepdims=True)
            weights = jnp.exp2((scores - top) * scale).astype(jnp.bfloat16)
            acc_ref[head, at, :] = jnp.dot(weights, value, preferred_element_type=jnp.float32)
            m_ref[head, at, :] = jnp.broadcast_to(top, (part, depth))

    def prepare(side, block):
        parts = [split(gather[block, s * tile_rows : (s + 1) * tile_rows, :]) for s in range(slots)]
        for head in range(kv_heads):
            kx[side, head] = jnp.concatenate([piece(p, 0, head) for p in parts], axis=0)
            vx[side, head, :, :depth] = jnp.concatenate([piece(p, 1, head) for p in parts], axis=0)

    def slot_live(slot):
        def look(at, found):
            return found | (table_ref[at] == slot).astype(jnp.int32)

        pages = table_ref.shape[0]
        if pages <= 16:
            found = jnp.int32(0)
            for at in range(pages):
                found = look(at, found)
            return found
        return lax.fori_loop(0, pages, look, jnp.int32(0))

    tile = min(128, rows * group)

    def prefix_part(side, block, head):
        columns = lax.broadcasted_iota(jnp.int32, (1, keys), 1)
        live = jnp.zeros((1, keys), jnp.int32)
        for s in range(slots):
            inside = (columns >= s * page) & (columns < (s + 1) * page)
            live = jnp.where(inside, slot_live(block * slots + s), live)
        for start in range(0, rows * group, tile):
            at = slice(start, start + tile)
            scores = lax.dot_general(
                qs[head, at, :], kx[side, head], (((1,), (1,)), ((), ())),
                preferred_element_type=jnp.float32,
            )
            scores = jnp.where(live > 0, scores, masked_score)
            before = m_ref[head, at, :]
            top = jnp.maximum(before, jnp.max(scores, axis=1, keepdims=True))
            factor = jnp.exp2((before - top) * scale)
            wide = top if keys == depth else top[:, :1]
            weights = jnp.exp2((scores - wide) * scale).astype(jnp.bfloat16)
            added = jnp.dot(weights, vx[side, head], preferred_element_type=jnp.float32)
            acc_ref[head, at, :depth] = acc_ref[head, at, :depth] * factor + added[:, :depth]
            acc_ref[head, at, depth:] = acc_ref[head, at, depth:] * factor + added[:, depth:]
            m_ref[head, at, :] = top

    def absorb(step, side, head):
        block = me - step if side == 0 else me + step

        @pl.when((block >= 0) & (block < n))
        def _():
            if head == 0:
                prepare(side, block)
            prefix_part(side, block, head)

    pieces = [(side, head) for side in range(2) for head in range(kv_heads)]

    for side in range(2):
        for head in range(kv_heads):
            vx[side, head, :, depth:] = jnp.ones((keys, depth), jnp.bfloat16)

    suffix_blocks = rows // SB
    early = suffix_blocks // 2
    late = (suffix_blocks - early) // chunks

    def run_suffix(first, count):
        def body(index, carry):
            suffix_block(first + index)
            return carry

        lax.fori_loop(0, count, body, 0, unroll=min(count, 2))

    run_suffix(0, suffix_blocks - late * chunks)
    copies[3].wait()
    for chunk in range(chunks):
        relay(1, chunk)
        run_suffix(suffix_blocks - late * (chunks - chunk), late)
    prepare(0, me)
    for head in range(kv_heads):
        prefix_part(0, me, head)

    def step_body(step):
        for chunk in range(chunks):
            relay(step, chunk)
            low = chunk * len(pieces) // chunks
            high = (chunk + 1) * len(pieces) // chunks
            for side, head in pieces[low:high]:
                absorb(step - 1, side, head)

    if n <= 8:
        for step in range(2, n):
            step_body(step)
    else:
        def loop(step, carry):
            step_body(step)
            return carry

        lax.fori_loop(2, n, loop, 0)
    for side, head in pieces:
        absorb(n - 1, side, head)

    quarter = rows * group // chunks
    span = rows // chunks
    count = count_ref[0]
    for chunk in range(chunks):
        at = pl.ds(chunk * quarter, quarter)
        heads_out = [
            (acc_ref[head, at, :depth] / acc_ref[head, at, depth:]).reshape(span, group, depth)
            for head in range(kv_heads)
        ]
        result = jnp.concatenate(heads_out, axis=1)
        row = lax.broadcasted_iota(jnp.int32, result.shape, 0) + chunk * span
        result = jnp.where(row < count, result, 0.0)
        out_ref[pl.ds(chunk * span, span)] = result.astype(jnp.bfloat16)

    def drain(block):
        for chunk in range(chunks):
            @pl.when(has_right & (block <= me))
            def _():
                send(0, block, chunk, False).wait_send()

            @pl.when(has_left & (block >= me))
            def _():
                send(1, block, chunk, False).wait_send()

    if n <= 8:
        for block in range(n):
            drain(block)
    else:
        def drain_loop(block, carry):
            drain(block)
            return carry

        lax.fori_loop(0, n, drain_loop, 0)


def store(held, out_hbm, sem):
    copy = pltpu.make_async_copy(held, out_hbm, sem)
    copy.start()
    copy.wait()


def shards(n, queries, prefix_pool, page_table, suffix_kv, new_kv, suffix_len, counts):
    rows, heads, depth = queries.shape
    slots, page, pair, kv_heads, depth = prefix_pool.shape
    suf_len = suffix_kv.shape[1]
    chunks = 4 if n <= 8 else 2
    group = heads // kv_heads
    dims = (rows, heads, kv_heads, depth, suf_len, page, slots, chunks)
    pool = prefix_pool.reshape(slots * page * 2 * kv_heads, depth)
    suffix = suffix_kv.reshape(rows * suf_len * 2 * kv_heads, depth)
    new = new_kv.reshape(rows * 2 * kv_heads, depth)
    tile_rows = page * 2 * kv_heads
    bf, f32 = jnp.bfloat16, jnp.float32
    anywhere = pl.BlockSpec(memory_space=pltpu.HBM)
    limit = 67043328 - rows * heads * depth * 2
    result = pl.pallas_call(
        functools.partial(kernel, n, dims),
        name="attend",
        out_shape=pltpu.VMEM((rows, heads, depth), bf),
        in_specs=[anywhere] * 7,
        out_specs=pl.BlockSpec(memory_space=pltpu.VMEM),
        scratch_shapes=[
            pltpu.SMEM(page_table.shape, jnp.int32),
            pltpu.SMEM(suffix_len.shape, jnp.int32),
            pltpu.SMEM(counts.shape, jnp.int32),
            pltpu.VMEM((n,) + pool.shape, bf),
            pltpu.VMEM(queries.shape, bf),
            pltpu.VMEM(suffix.shape, bf),
            pltpu.VMEM(new.shape, bf),
            pltpu.VMEM((tile_rows, tile_rows), bf),
            pltpu.VMEM((kv_heads, rows * group, depth), bf),
            pltpu.VMEM((kv_heads, rows, depth), bf),
            pltpu.VMEM((kv_heads, rows, depth), bf),
            pltpu.VMEM((2, kv_heads, slots * page, depth), bf),
            pltpu.VMEM((2, kv_heads, slots * page, 2 * depth), bf),
            pltpu.VMEM((kv_heads, rows * group, depth), f32),
            pltpu.VMEM((kv_heads, rows * group, 2 * depth), f32),
            pltpu.SemaphoreType.DMA((7,)),
            pltpu.SemaphoreType.DMA((2, n, chunks)),
            pltpu.SemaphoreType.DMA((n, chunks)),
        ],
        compiler_params=pltpu.CompilerParams(
            collective_id=0, has_side_effects=True, vmem_limit_bytes=limit
        ),
    )(page_table, suffix_len, counts, queries, pool, suffix, new)
    return pl.pallas_call(
        store,
        name="store",
        out_shape=jax.ShapeDtypeStruct((rows, heads, depth), bf),
        in_specs=[pl.BlockSpec(memory_space=pltpu.VMEM)],
        out_specs=pl.BlockSpec(memory_space=pltpu.HBM),
        scratch_shapes=[pltpu.SemaphoreType.DMA],
        compiler_params=pltpu.CompilerParams(vmem_limit_bytes=4 * 2**20),
    )(result)


def solution(mesh):
    placed = (
        P(("groups", "replica"), "tensor", None),
        P(("groups", "replica"), None, None, "tensor", None),
        P("groups"),
        P(("groups", "replica"), None, None, "tensor", None),
        P(("groups", "replica"), None, "tensor", None),
        P(("groups", "replica")),
        P(("groups", "replica")),
    )
    return jax.shard_map(
        functools.partial(shards, mesh.shape["replica"]),
        mesh=mesh,
        in_specs=placed,
        out_specs=P(("groups", "replica"), "tensor", None),
        check_vma=False,
    )
```

```python
import functools
import math

import jax
import jax.numpy as jnp
from jax import lax
from jax.experimental import pallas as pl
from jax.experimental.pallas import tpu as pltpu
from jax.sharding import PartitionSpec as P

masked_score = -1e30
MESH = pl.DeviceIdType.MESH
SB = 8


def kernel(n, dims, table_hbm, len_hbm, count_hbm, q_hbm, pool_hbm, suf_hbm, new_hbm, out_ref,
           table_ref, len_ref, count_ref, gather, q_in, suf, new, perm, qs, knew, vnew, m_ref, acc_ref,
           local_sem, send_sem, recv_sem):
    rows, heads, kv_heads, depth, suf_len, page, slots, chunks = dims
    group = heads // kv_heads
    per_token = 2 * kv_heads
    scale = (1.0 / math.sqrt(depth)) * math.log2(math.e)
    block_rows = slots * page * per_token
    chunk_rows = block_rows // chunks
    tile_tokens = page
    tile_rows = page * per_token
    keys = slots * page
    me = lax.axis_index("replica")
    has_left, has_right = me > 0, me < n - 1

    barrier = pltpu.get_barrier_semaphore()

    @pl.when(has_left)
    def _():
        pl.semaphore_signal(barrier, inc=1, device_id={"replica": me - 1}, device_id_type=MESH)

    @pl.when(has_right)
    def _():
        pl.semaphore_signal(barrier, inc=1, device_id={"replica": me + 1}, device_id_type=MESH)

    copies = [
        pltpu.make_async_copy(q_hbm, q_in, local_sem.at[0]),
        pltpu.make_async_copy(new_hbm, new, local_sem.at[1]),
        pltpu.make_async_copy(suf_hbm, suf, local_sem.at[2]),
        pltpu.make_async_copy(pool_hbm, gather.at[me], local_sem.at[3]),
        pltpu.make_async_copy(table_hbm, table_ref, local_sem.at[4]),
        pltpu.make_async_copy(len_hbm, len_ref, local_sem.at[5]),
        pltpu.make_async_copy(count_hbm, count_ref, local_sem.at[6]),
    ]
    for copy in copies:
        copy.start()

    out_row = lax.broadcasted_iota(jnp.int32, (tile_rows, tile_rows), 0)
    in_row = lax.broadcasted_iota(jnp.int32, (tile_rows, tile_rows), 1)
    source = lax.rem(out_row, page) * per_token + lax.div(out_row, page)
    perm[...] = jnp.where(in_row == source, 1.0, 0.0).astype(jnp.bfloat16)

    pl.semaphore_wait(barrier, has_left.astype(jnp.int32) + has_right.astype(jnp.int32))

    def send(direction, block, chunk, own):
        at = pl.ds(chunk * chunk_rows, chunk_rows)
        return pltpu.make_async_remote_copy(
            src_ref=pool_hbm.at[at] if own else gather.at[block, at],
            dst_ref=gather.at[block, at],
            send_sem=send_sem.at[direction, block, chunk],
            recv_sem=recv_sem.at[block, chunk],
            device_id={"replica": me + 1 if direction == 0 else me - 1},
            device_id_type=MESH,
        )

    for chunk in range(chunks):
        @pl.when(has_right)
        def _():
            send(0, me, chunk, True).start()

        @pl.when(has_left)
        def _():
            send(1, me, chunk, True).start()

    def relay(step, chunk):
        @pl.when(me - step >= 0)
        def _():
            send(0, me - step, chunk, False).wait_recv()

            @pl.when(has_right)
            def _():
                send(0, me - step, chunk, False).start()

        @pl.when(me + step < n)
        def _():
            send(1, me + step, chunk, False).wait_recv()

            @pl.when(has_left)
            def _():
                send(1, me + step, chunk, False).start()

    def split(block):
        return jnp.dot(perm[...], block, preferred_element_type=jnp.float32).astype(jnp.bfloat16)

    def piece(parts, which, head):
        at = (which * kv_heads + head) * page
        return parts[at : at + page]

    copies[0].wait()
    copies[1].wait()
    queries = q_in[...].astype(jnp.float32).reshape(rows, kv_heads, group, depth)
    for head in range(kv_heads):
        qs[head] = queries[:, head].reshape(rows * group, depth).astype(jnp.bfloat16)
    fresh = split(new[...])
    for head in range(kv_heads):
        knew[head] = piece(fresh, 0, head)
        vnew[head] = piece(fresh, 1, head)
    copies[2].wait()
    for copy in copies[4:]:
        copy.wait()

    block_keys = SB * suf_len
    width = block_keys + rows
    tiles = block_keys // tile_tokens
    part = SB * group

    def suffix_block(index):
        columns = lax.broadcasted_iota(jnp.int32, (group, width), 1)
        masks = []
        for at in range(SB):
            low = at * suf_len
            high = low + len_ref[index * SB + at]
            own = (columns >= low) & (columns < high)
            masks.append(own | (columns == block_keys + index * SB + at))
        parts = [
            split(suf[pl.ds(pl.multiple_of((index * tiles + t) * tile_rows, tile_rows), tile_rows), :])
            for t in range(tiles)
        ]
        ones = jnp.ones((width, depth), jnp.bfloat16)
        at = pl.ds(pl.multiple_of(index * part, part), part)
        for head in range(kv_heads):
            key = jnp.concatenate([piece(p, 0, head) for p in parts] + [knew[head]], axis=0)
            value = jnp.concatenate([piece(p, 1, head) for p in parts] + [vnew[head]], axis=0)
            value = jnp.concatenate([value, ones], axis=1)
            scores = lax.dot_general(
                qs[head, at, :], key, (((1,), (1,)), ((), ())), preferred_element_type=jnp.float32
            )
            scores = jnp.concatenate(
                [
                    jnp.where(masks[i], scores[i * group : (i + 1) * group], masked_score)
                    for i in range(SB)
                ],
                axis=0,
            )
            top = jnp.max(scores, axis=1, keepdims=True)
            weights = jnp.exp2((scores - top) * scale).astype(jnp.bfloat16)
            acc_ref[head, at, :] = jnp.dot(weights, value, preferred_element_type=jnp.float32)
            m_ref[head, at, :] = jnp.broadcast_to(top, (part, depth))

    def slot_live(slot):
        def look(at, found):
            return found | (table_ref[at] == slot).astype(jnp.int32)

        pages = table_ref.shape[0]
        if pages <= 16:
            found = jnp.int32(0)
            for at in range(pages):
                found = look(at, found)
            return found
        return lax.fori_loop(0, pages, look, jnp.int32(0))

    tile = min(128, rows * group)

    def absorb_block(block):
        columns = lax.broadcasted_iota(jnp.int32, (1, keys), 1)
        live = jnp.zeros((1, keys), jnp.int32)
        for s in range(slots):
            inside = (columns >= s * page) & (columns < (s + 1) * page)
            live = jnp.where(inside, slot_live(block * slots + s), live)
        parts = [split(gather[block, s * tile_rows : (s + 1) * tile_rows, :]) for s in range(slots)]
        ones = jnp.ones((keys, depth), jnp.bfloat16)
        for head in range(kv_heads):
            key = jnp.concatenate([piece(p, 0, head) for p in parts], axis=0)
            value = jnp.concatenate([piece(p, 1, head) for p in parts], axis=0)
            value = jnp.concatenate([value, ones], axis=1)
            for start in range(0, rows * group, tile):
                at = slice(start, start + tile)
                scores = lax.dot_general(
                    qs[head, at, :], key, (((1,), (1,)), ((), ())),
                    preferred_element_type=jnp.float32,
                )
                scores = jnp.where(live > 0, scores, masked_score)
                before = m_ref[head, at, :]
                top = jnp.maximum(before, jnp.max(scores, axis=1, keepdims=True))
                factor = jnp.exp2((before - top) * scale)
                wide = top if keys == depth else top[:, :1]
                weights = jnp.exp2((scores - wide) * scale).astype(jnp.bfloat16)
                added = jnp.dot(weights, value, preferred_element_type=jnp.float32)
                acc_ref[head, at, :depth] = acc_ref[head, at, :depth] * factor + added[:, :depth]
                acc_ref[head, at, depth:] = acc_ref[head, at, depth:] * factor + added[:, depth:]
                m_ref[head, at, :] = top

    def absorb(step):
        for block in (me - step, me + step):
            @pl.when((block >= 0) & (block < n))
            def _():
                absorb_block(block)

    suffix_blocks = rows // SB
    early = suffix_blocks // 2
    late = (suffix_blocks - early) // chunks

    def run_suffix(first, count):
        def body(index, carry):
            suffix_block(first + index)
            return carry

        lax.fori_loop(0, count, body, 0, unroll=min(count, 2))

    run_suffix(0, suffix_blocks - late * chunks)
    copies[3].wait()
    for chunk in range(chunks):
        relay(1, chunk)
        run_suffix(suffix_blocks - late * (chunks - chunk), late)
    absorb_block(me)

    def forward(step):
        for chunk in range(chunks):
            relay(step, chunk)

    if n > 2:
        forward(2)
    absorb(1)
    if n > 2:
        absorb(2)

    def step_body(step, carry):
        forward(step)
        absorb(step)
        return carry

    if n <= 8:
        for step in range(3, n):
            step_body(step, 0)
    else:
        lax.fori_loop(3, n, step_body, 0)

    quarter = rows * group // chunks
    span = rows // chunks
    count = count_ref[0]
    for chunk in range(chunks):
        at = pl.ds(chunk * quarter, quarter)
        heads_out = [
            (acc_ref[head, at, :depth] / acc_ref[head, at, depth:]).reshape(span, group, depth)
            for head in range(kv_heads)
        ]
        result = jnp.concatenate(heads_out, axis=1)
        row = lax.broadcasted_iota(jnp.int32, result.shape, 0) + chunk * span
        result = jnp.where(row < count, result, 0.0)
        out_ref[pl.ds(chunk * span, span)] = result.astype(jnp.bfloat16)

    def drain(block):
        for chunk in range(chunks):
            @pl.when(has_right & (block <= me))
            def _():
                send(0, block, chunk, False).wait_send()

            @pl.when(has_left & (block >= me))
            def _():
                send(1, block, chunk, False).wait_send()

    if n <= 8:
        for block in range(n):
            drain(block)
    else:
        def drain_loop(block, carry):
            drain(block)
            return carry

        lax.fori_loop(0, n, drain_loop, 0)


def store(held, out_hbm, sem):
    copy = pltpu.make_async_copy(held, out_hbm, sem)
    copy.start()
    copy.wait()


def shards(n, queries, prefix_pool, page_table, suffix_kv, new_kv, suffix_len, counts):
    rows, heads, depth = queries.shape
    slots, page, pair, kv_heads, depth = prefix_pool.shape
    suf_len = suffix_kv.shape[1]
    chunks = 4 if n <= 8 else 2
    group = heads // kv_heads
    dims = (rows, heads, kv_heads, depth, suf_len, page, slots, chunks)
    pool = prefix_pool.reshape(slots * page * 2 * kv_heads, depth)
    suffix = suffix_kv.reshape(rows * suf_len * 2 * kv_heads, depth)
    new = new_kv.reshape(rows * 2 * kv_heads, depth)
    tile_rows = page * 2 * kv_heads
    bf, f32 = jnp.bfloat16, jnp.float32
    anywhere = pl.BlockSpec(memory_space=pltpu.HBM)
    limit = 67043328 - rows * heads * depth * 2
    result = pl.pallas_call(
        functools.partial(kernel, n, dims),
        name="attend",
        out_shape=pltpu.VMEM((rows, heads, depth), bf),
        in_specs=[anywhere] * 7,
        out_specs=pl.BlockSpec(memory_space=pltpu.VMEM),
        scratch_shapes=[
            pltpu.SMEM(page_table.shape, jnp.int32),
            pltpu.SMEM(suffix_len.shape, jnp.int32),
            pltpu.SMEM(counts.shape, jnp.int32),
            pltpu.VMEM((n,) + pool.shape, bf),
            pltpu.VMEM(queries.shape, bf),
            pltpu.VMEM(suffix.shape, bf),
            pltpu.VMEM(new.shape, bf),
            pltpu.VMEM((tile_rows, tile_rows), bf),
            pltpu.VMEM((kv_heads, rows * group, depth), bf),
            pltpu.VMEM((kv_heads, rows, depth), bf),
            pltpu.VMEM((kv_heads, rows, depth), bf),
            pltpu.VMEM((kv_heads, rows * group, depth), f32),
            pltpu.VMEM((kv_heads, rows * group, 2 * depth), f32),
            pltpu.SemaphoreType.DMA((7,)),
            pltpu.SemaphoreType.DMA((2, n, chunks)),
            pltpu.SemaphoreType.DMA((n, chunks)),
        ],
        compiler_params=pltpu.CompilerParams(
            collective_id=0, has_side_effects=True, vmem_limit_bytes=limit
        ),
    )(page_table, suffix_len, counts, queries, pool, suffix, new)
    return pl.pallas_call(
        store,
        name="store",
        out_shape=jax.ShapeDtypeStruct((rows, heads, depth), bf),
        in_specs=[pl.BlockSpec(memory_space=pltpu.VMEM)],
        out_specs=pl.BlockSpec(memory_space=pltpu.HBM),
        scratch_shapes=[pltpu.SemaphoreType.DMA],
        compiler_params=pltpu.CompilerParams(vmem_limit_bytes=4 * 2**20),
    )(result)


def solution(mesh):
    placed = (
        P(("groups", "replica"), "tensor", None),
        P(("groups", "replica"), None, None, "tensor", None),
        P("groups"),
        P(("groups", "replica"), None, None, "tensor", None),
        P(("groups", "replica"), None, "tensor", None),
        P(("groups", "replica")),
        P(("groups", "replica")),
    )
    return jax.shard_map(
        functools.partial(shards, mesh.shape["replica"]),
        mesh=mesh,
        in_specs=placed,
        out_specs=P(("groups", "replica"), "tensor", None),
        check_vma=False,
    )
```

```python
import functools
import math

import jax
import jax.numpy as jnp
from jax import lax
from jax.experimental import pallas as pl
from jax.experimental.pallas import tpu as pltpu
from jax.sharding import PartitionSpec as P

masked_score = -1e30
MESH = pl.DeviceIdType.MESH
SB = 8


def kernel(n, dims, table_hbm, len_hbm, count_hbm, q_hbm, pool_hbm, suf_hbm, new_hbm, out_ref,
           table_ref, len_ref, count_ref, gather, q_in, suf, new, perm, qs, knew, vnew, m_ref, acc_ref,
           local_sem, send_sem, recv_sem):
    rows, heads, kv_heads, depth, suf_len, page, slots, chunks = dims
    group = heads // kv_heads
    per_token = 2 * kv_heads
    scale = (1.0 / math.sqrt(depth)) * math.log2(math.e)
    block_rows = slots * page * per_token
    chunk_rows = block_rows // chunks
    tile_tokens = page
    tile_rows = page * per_token
    keys = slots * page
    me = lax.axis_index("replica")
    has_left, has_right = me > 0, me < n - 1

    barrier = pltpu.get_barrier_semaphore()

    @pl.when(has_left)
    def _():
        pl.semaphore_signal(barrier, inc=1, device_id={"replica": me - 1}, device_id_type=MESH)

    @pl.when(has_right)
    def _():
        pl.semaphore_signal(barrier, inc=1, device_id={"replica": me + 1}, device_id_type=MESH)

    copies = [
        pltpu.make_async_copy(q_hbm, q_in, local_sem.at[0]),
        pltpu.make_async_copy(new_hbm, new, local_sem.at[1]),
        pltpu.make_async_copy(suf_hbm, suf, local_sem.at[2]),
        pltpu.make_async_copy(pool_hbm, gather.at[me], local_sem.at[3]),
        pltpu.make_async_copy(table_hbm, table_ref, local_sem.at[4]),
        pltpu.make_async_copy(len_hbm, len_ref, local_sem.at[5]),
        pltpu.make_async_copy(count_hbm, count_ref, local_sem.at[6]),
    ]
    for copy in copies:
        copy.start()

    out_row = lax.broadcasted_iota(jnp.int32, (tile_rows, tile_rows), 0)
    in_row = lax.broadcasted_iota(jnp.int32, (tile_rows, tile_rows), 1)
    source = lax.rem(out_row, page) * per_token + lax.div(out_row, page)
    perm[...] = jnp.where(in_row == source, 1.0, 0.0).astype(jnp.bfloat16)

    pl.semaphore_wait(barrier, has_left.astype(jnp.int32) + has_right.astype(jnp.int32))

    def send(direction, block, chunk, own):
        at = pl.ds(chunk * chunk_rows, chunk_rows)
        return pltpu.make_async_remote_copy(
            src_ref=pool_hbm.at[at] if own else gather.at[block, at],
            dst_ref=gather.at[block, at],
            send_sem=send_sem.at[direction, block, chunk],
            recv_sem=recv_sem.at[block, chunk],
            device_id={"replica": me + 1 if direction == 0 else me - 1},
            device_id_type=MESH,
        )

    for chunk in range(chunks):
        @pl.when(has_right)
        def _():
            send(0, me, chunk, True).start()

        @pl.when(has_left)
        def _():
            send(1, me, chunk, True).start()

    def relay(step, chunk):
        @pl.when(me - step >= 0)
        def _():
            send(0, me - step, chunk, False).wait_recv()

            @pl.when(has_right)
            def _():
                send(0, me - step, chunk, False).start()

        @pl.when(me + step < n)
        def _():
            send(1, me + step, chunk, False).wait_recv()

            @pl.when(has_left)
            def _():
                send(1, me + step, chunk, False).start()

    def split(block):
        return jnp.dot(perm[...], block, preferred_element_type=jnp.float32).astype(jnp.bfloat16)

    def piece(parts, which, head):
        at = (which * kv_heads + head) * page
        return parts[at : at + page]

    copies[0].wait()
    copies[1].wait()
    queries = q_in[...].astype(jnp.float32).reshape(rows, kv_heads, group, depth)
    for head in range(kv_heads):
        qs[head] = queries[:, head].reshape(rows * group, depth).astype(jnp.bfloat16)
    fresh = split(new[...])
    for head in range(kv_heads):
        knew[head] = piece(fresh, 0, head)
        vnew[head] = piece(fresh, 1, head)
    copies[2].wait()
    for copy in copies[4:]:
        copy.wait()

    block_keys = SB * suf_len
    width = block_keys + rows
    tiles = block_keys // tile_tokens
    part = SB * group

    def suffix_block(index):
        columns = lax.broadcasted_iota(jnp.int32, (group, width), 1)
        masks = []
        for at in range(SB):
            low = at * suf_len
            high = low + len_ref[index * SB + at]
            own = (columns >= low) & (columns < high)
            masks.append(own | (columns == block_keys + index * SB + at))
        parts = [
            split(suf[pl.ds(pl.multiple_of((index * tiles + t) * tile_rows, tile_rows), tile_rows), :])
            for t in range(tiles)
        ]
        ones = jnp.ones((width, depth), jnp.bfloat16)
        at = pl.ds(pl.multiple_of(index * part, part), part)
        for head in range(kv_heads):
            key = jnp.concatenate([piece(p, 0, head) for p in parts] + [knew[head]], axis=0)
            value = jnp.concatenate([piece(p, 1, head) for p in parts] + [vnew[head]], axis=0)
            value = jnp.concatenate([value, ones], axis=1)
            scores = lax.dot_general(
                qs[head, at, :], key, (((1,), (1,)), ((), ())), preferred_element_type=jnp.float32
            )
            scores = jnp.concatenate(
                [
                    jnp.where(masks[i], scores[i * group : (i + 1) * group], masked_score)
                    for i in range(SB)
                ],
                axis=0,
            )
            top = jnp.max(scores, axis=1, keepdims=True)
            weights = jnp.exp2((scores - top) * scale).astype(jnp.bfloat16)
            acc_ref[head, at, :] = jnp.dot(weights, value, preferred_element_type=jnp.float32)
            m_ref[head, at, :] = jnp.broadcast_to(top, (part, depth))

    def slot_live(slot):
        def look(at, found):
            return found | (table_ref[at] == slot).astype(jnp.int32)

        pages = table_ref.shape[0]
        if pages <= 16:
            found = jnp.int32(0)
            for at in range(pages):
                found = look(at, found)
            return found
        return lax.fori_loop(0, pages, look, jnp.int32(0))

    tile = min(128, rows * group)

    def absorb_block(block):
        columns = lax.broadcasted_iota(jnp.int32, (1, keys), 1)
        live = jnp.zeros((1, keys), jnp.int32)
        for s in range(slots):
            inside = (columns >= s * page) & (columns < (s + 1) * page)
            live = jnp.where(inside, slot_live(block * slots + s), live)
        parts = [split(gather[block, s * tile_rows : (s + 1) * tile_rows, :]) for s in range(slots)]
        ones = jnp.ones((keys, depth), jnp.bfloat16)
        for head in range(kv_heads):
            key = jnp.concatenate([piece(p, 0, head) for p in parts], axis=0)
            value = jnp.concatenate([piece(p, 1, head) for p in parts], axis=0)
            value = jnp.concatenate([value, ones], axis=1)
            for start in range(0, rows * group, tile):
                at = slice(start, start + tile)
                scores = lax.dot_general(
                    qs[head, at, :], key, (((1,), (1,)), ((), ())),
                    preferred_element_type=jnp.float32,
                )
                scores = jnp.where(live > 0, scores, masked_score)
                before = m_ref[head, at, :]
                top = jnp.maximum(before, jnp.max(scores, axis=1, keepdims=True))
                factor = jnp.exp2((before - top) * scale)
                wide = top if keys == depth else top[:, :1]
                weights = jnp.exp2((scores - wide) * scale).astype(jnp.bfloat16)
                added = jnp.dot(weights, value, preferred_element_type=jnp.float32)
                acc_ref[head, at, :depth] = acc_ref[head, at, :depth] * factor + added[:, :depth]
                acc_ref[head, at, depth:] = acc_ref[head, at, depth:] * factor + added[:, depth:]
                m_ref[head, at, :] = top

    def absorb(step):
        for block in (me - step, me + step):
            @pl.when((block >= 0) & (block < n))
            def _():
                absorb_block(block)

    suffix_blocks = rows // SB
    early = suffix_blocks // 2
    late = (suffix_blocks - early) // chunks

    def run_suffix(first, count):
        def body(index, carry):
            suffix_block(first + index)
            return carry

        lax.fori_loop(0, count, body, 0, unroll=min(count, 4))

    run_suffix(0, suffix_blocks - late * chunks)
    copies[3].wait()
    for chunk in range(chunks):
        relay(1, chunk)
        run_suffix(suffix_blocks - late * (chunks - chunk), late)
    absorb_block(me)

    def forward(step):
        for chunk in range(chunks):
            relay(step, chunk)

    if n > 2:
        forward(2)
    absorb(1)
    if n > 2:
        absorb(2)

    def step_body(step, carry):
        forward(step)
        absorb(step)
        return carry

    if n <= 8:
        for step in range(3, n):
            step_body(step, 0)
    else:
        lax.fori_loop(3, n, step_body, 0)

    quarter = rows * group // chunks
    span = rows // chunks
    count = count_ref[0]
    for chunk in range(chunks):
        at = pl.ds(chunk * quarter, quarter)
        heads_out = [
            (acc_ref[head, at, :depth] / acc_ref[head, at, depth:]).reshape(span, group, depth)
            for head in range(kv_heads)
        ]
        result = jnp.concatenate(heads_out, axis=1)
        row = lax.broadcasted_iota(jnp.int32, result.shape, 0) + chunk * span
        result = jnp.where(row < count, result, 0.0)
        out_ref[pl.ds(chunk * span, span)] = result.astype(jnp.bfloat16)

    def drain(block):
        for chunk in range(chunks):
            @pl.when(has_right & (block <= me))
            def _():
                send(0, block, chunk, False).wait_send()

            @pl.when(has_left & (block >= me))
            def _():
                send(1, block, chunk, False).wait_send()

    if n <= 8:
        for block in range(n):
            drain(block)
    else:
        def drain_loop(block, carry):
            drain(block)
            return carry

        lax.fori_loop(0, n, drain_loop, 0)


def store(held, out_hbm, sem):
    copy = pltpu.make_async_copy(held, out_hbm, sem)
    copy.start()
    copy.wait()


def shards(n, queries, prefix_pool, page_table, suffix_kv, new_kv, suffix_len, counts):
    rows, heads, depth = queries.shape
    slots, page, pair, kv_heads, depth = prefix_pool.shape
    suf_len = suffix_kv.shape[1]
    chunks = 4 if n <= 8 else 2
    group = heads // kv_heads
    dims = (rows, heads, kv_heads, depth, suf_len, page, slots, chunks)
    pool = prefix_pool.reshape(slots * page * 2 * kv_heads, depth)
    suffix = suffix_kv.reshape(rows * suf_len * 2 * kv_heads, depth)
    new = new_kv.reshape(rows * 2 * kv_heads, depth)
    tile_rows = page * 2 * kv_heads
    bf, f32 = jnp.bfloat16, jnp.float32
    anywhere = pl.BlockSpec(memory_space=pltpu.HBM)
    limit = 67043328 - rows * heads * depth * 2
    result = pl.pallas_call(
        functools.partial(kernel, n, dims),
        name="attend",
        out_shape=pltpu.VMEM((rows, heads, depth), bf),
        in_specs=[anywhere] * 7,
        out_specs=pl.BlockSpec(memory_space=pltpu.VMEM),
        scratch_shapes=[
            pltpu.SMEM(page_table.shape, jnp.int32),
            pltpu.SMEM(suffix_len.shape, jnp.int32),
            pltpu.SMEM(counts.shape, jnp.int32),
            pltpu.VMEM((n,) + pool.shape, bf),
            pltpu.VMEM(queries.shape, bf),
            pltpu.VMEM(suffix.shape, bf),
            pltpu.VMEM(new.shape, bf),
            pltpu.VMEM((tile_rows, tile_rows), bf),
            pltpu.VMEM((kv_heads, rows * group, depth), bf),
            pltpu.VMEM((kv_heads, rows, depth), bf),
            pltpu.VMEM((kv_heads, rows, depth), bf),
            pltpu.VMEM((kv_heads, rows * group, depth), f32),
            pltpu.VMEM((kv_heads, rows * group, 2 * depth), f32),
            pltpu.SemaphoreType.DMA((7,)),
            pltpu.SemaphoreType.DMA((2, n, chunks)),
            pltpu.SemaphoreType.DMA((n, chunks)),
        ],
        compiler_params=pltpu.CompilerParams(
            collective_id=0, has_side_effects=True, vmem_limit_bytes=limit
        ),
    )(page_table, suffix_len, counts, queries, pool, suffix, new)
    return pl.pallas_call(
        store,
        name="store",
        out_shape=jax.ShapeDtypeStruct((rows, heads, depth), bf),
        in_specs=[pl.BlockSpec(memory_space=pltpu.VMEM)],
        out_specs=pl.BlockSpec(memory_space=pltpu.HBM),
        scratch_shapes=[pltpu.SemaphoreType.DMA],
        compiler_params=pltpu.CompilerParams(vmem_limit_bytes=4 * 2**20),
    )(result)


def solution(mesh):
    placed = (
        P(("groups", "replica"), "tensor", None),
        P(("groups", "replica"), None, None, "tensor", None),
        P("groups"),
        P(("groups", "replica"), None, None, "tensor", None),
        P(("groups", "replica"), None, "tensor", None),
        P(("groups", "replica")),
        P(("groups", "replica")),
    )
    return jax.shard_map(
        functools.partial(shards, mesh.shape["replica"]),
        mesh=mesh,
        in_specs=placed,
        out_specs=P(("groups", "replica"), "tensor", None),
        check_vma=False,
    )
```
